32 devices in a mesh: dp: 8 (over z, y), db: 4 (over x, core).
Axes of the slice: x: 2, y: 2, z: 4, core: 2. Of those that a mesh axis runs over, the one named last changes fastest.
Arguments:
- queries: bfloat16 [8, 1024, 2048], P('dp', 'db'), may hold values from -6 to 6
- cotangent: bfloat16 [8, 1024, 2048], P('dp', 'db'), may hold values from -6 to 6
- w_key: bfloat16 [896, 2048], replicated, may hold values from -0.1875 to 0.1875
- w_value: bfloat16 [896, 2048], replicated, may hold values from -0.1875 to 0.1875
- database: bfloat16 [128, 128, 896], P('db'), may hold values from -6 to 6
- nb_shard: int32 [8, 16, 2], P('dp', 'db'), may hold values from 0 to 3, all different within a row; in each aligned block of 4 rows (0 to 3, 4 to 7, ..., all dimensions but the last counted through in order) at most 3 rows name the same one
- nb_row: int32 [8, 16, 2], P('dp', 'db'), may hold values from 0 to 31
Outputs:
- attn_out: bfloat16 [8, 1024, 2048], P('dp', 'db')
- grad_queries: bfloat16 [8, 1024, 2048], P('dp', 'db')
- grad_wkey: float32 [896, 2048], P(('dp', 'db'))
- grad_wvalue: float32 [896, 2048], P(('dp', 'db'))
- grad_database: bfloat16 [128, 128, 896], P('db', 'dp')
The draws below stay inside these ranges and needn't reach their ends.
Inputs may be any that keep to these rules, and one draw needn't show every extreme that they name: `nb_shard`: the 2 neighbours of a stretch lie on different shards; among the stretches of one device (aligned blocks of 4 stretches of a sequence) at most 3 name the same shard, a bound that some block reaches.
All inputs are finite; a program needn't handle non-finite values.
Results may differ from the reference program's by a relative error of at most 0.015.
Values may be sent and summed in bfloat16 or wider, within the bound.
A program may use at most 192 MiB of HBM per device.

```python
import math
import jax
import jax.numpy as jnp
import numpy as np
from jax import lax

HEADS = 16
HSIZE = 128
ENC = 896
STRETCH = 64
NEIGH = 2
NB_LEN = 128
CH_DEV = 4
DB_DEV = 32
HD = 2048
SEQS = 8
LENGTH = 1024
STRETCHES = 16
DB = 128
CAP = 3
N_DB = 4


def plant(drawn, own_key, least, high):
    extent = drawn.shape
    spot = [jax.random.randint(jax.random.fold_in(own_key, axis), (), 0, extent[axis]) for axis in range(len(extent))]
    drawn = drawn.at[tuple(spot)].set(least)
    longest = extent.index(max(extent))
    spot[longest] = (spot[longest] + 1) % extent[longest]
    return drawn.at[tuple(spot)].set(high)


def block_levels(own_key, extent, split, low, top_value):
    def one(position, blocks):
        draws = jax.random.uniform(jax.random.fold_in(jax.random.fold_in(own_key, 6), position), (blocks,), jnp.float32, low / len(split), top_value / len(split))
        return jnp.repeat(jnp.exp(draws), extent[position] // blocks).reshape((-1,) + (1,) * (len(extent) - position - 1))

    level = one(*split[0])
    for cut in split[1:]:
        level = level * one(*cut)
    return level


def assign_block(key, own, number, rows, count, top, bound, skew):
    order = jax.random.permutation(key, count)
    crowded, usual = load_shares(count, rows * top, bound, skew, True), load_shares(count, rows * top, bound, skew, False)
    places = jnp.arange(count)

    def named(tallies, turn):
        used = int((tallies > 0).sum())
        fixed = max(1, used // 4)
        moved = fixed + (places - fixed + turn * (used - fixed)) % max(1, count - fixed)
        return jnp.zeros((count,), jnp.int32).at[order[jnp.where(places < fixed, places, moved)]].set(jnp.asarray(tallies, jnp.int32))

    tallies = jnp.where(number % 4 == 0, named(crowded, number // 4), named(usual, number - number // 4 - 1))
    mixed = jax.random.permutation(jax.random.fold_in(own, 3), count)
    donor, receiver = mixed[0:count // 2 * 2:2], mixed[1:count // 2 * 2:2]
    slack = jnp.minimum(tallies[donor] - 1, bound - tallies[receiver]) // 2
    slack = jnp.where((donor == order[0]) | (receiver == order[0]) | (tallies[receiver] == 0), 0, jnp.maximum(slack, 0))
    moved = jax.random.randint(jax.random.fold_in(own, 4), (count // 2,), 0, 1 << 20) % (slack + 1)
    tallies = tallies.at[donor].add(-moved).at[receiver].add(moved)
    items = jnp.searchsorted(jnp.cumsum(tallies), jnp.arange(rows * top), side="right").astype(jnp.int32)
    grid = items.reshape(top, rows).T
    grid = grid[jax.random.permutation(jax.random.fold_in(own, 1), rows)]
    turn = jax.random.randint(jax.random.fold_in(own, 2), (rows, 1), 0, top)
    return jnp.take_along_axis(grid, (jnp.arange(top)[None, :] + turn) % top, axis=1)


def load_shares(count, total, most, lean, full):
    weights = [(1 << 20) // math.isqrt(standing ** lean) + 1 for standing in range(1, count + 1)]
    largest = most if full else min(most, max(-(-total // count), total * weights[0] // sum(weights)))
    least = 1 if total - largest >= count - 1 else 0
    counts, rest = [largest] + [least] * (count - 1), total - largest - least * (count - 1)
    while rest > 0:
        candidates = [i for i in range(1, count) if counts[i] < largest] or [i for i in range(1, count) if counts[i] < most]
        mass, remaining = sum([weights[i] for i in candidates]), rest
        for i in candidates:
            extra = min(most - counts[i], max(1, remaining * weights[i] // mass), rest)
            counts[i] = counts[i] + extra
            rest = rest - extra
    return np.array(counts)


def noise(own_key, extent, spread, most, shards=(), held_as=jnp.bfloat16):
    array = spread * jax.random.normal(own_key, extent, jnp.float32)
    if shards:
        array = array * block_levels(own_key, extent, shards, -0.22, 0.18)
    return jnp.clip(array, -most, most).astype(held_as)


def setup_inputs(seed: int = 0) -> dict:
    seeds = jax.random.split(jax.random.key(seed), 8)
    queries = noise(seeds[0], (SEQS, LENGTH, HD), 1.0, 6.0, ((0, 8), (1, 4)))
    cotangent = noise(seeds[1], (SEQS, LENGTH, HD), 1.0, 6.0, ((0, 8), (1, 4)))
    w_key = noise(seeds[2], (ENC, HD), ENC ** -0.5, 0.1875)
    w_value = noise(seeds[3], (ENC, HD), ENC ** -0.5, 0.1875)
    database = noise(seeds[4], (DB, NB_LEN, ENC), 1.0, 6.0, ((0, 4),))
    nb_shard_keys = jax.random.split(jax.random.fold_in(seeds[5], 1), SEQS * STRETCHES // CH_DEV)
    nb_shard_turns = jax.random.permutation(jax.random.fold_in(seeds[5], 3), SEQS * STRETCHES // CH_DEV)
    nb_shard = jax.vmap(lambda own, number: assign_block(jax.random.fold_in(seeds[5], 2), own, number, CH_DEV, N_DB, NEIGH, CAP, 2))(nb_shard_keys, nb_shard_turns).reshape((SEQS, STRETCHES, NEIGH))
    nb_row = plant(jax.random.randint(seeds[6], (SEQS, STRETCHES, NEIGH), 0, DB_DEV), jax.random.fold_in(seeds[6], 1), 0, DB_DEV - 1).astype(jnp.int32)
    return {"queries": queries, "cotangent": cotangent, "w_key": w_key, "w_value": w_value, "database": database, "nb_shard": nb_shard, "nb_row": nb_row}


def attend_blocks(block_q, block_g, states, w_key, w_value):
    blocks, length, width = block_q.shape
    span = states.shape[1]
    head_size = width // HEADS
    scale = 1.0 / math.sqrt(head_size)
    keys = jnp.einsum('bre,ef->brf', states.astype(jnp.float32), w_key.astype(jnp.float32)).astype(jnp.bfloat16)
    values = jnp.einsum('bre,ef->brf', states.astype(jnp.float32), w_value.astype(jnp.float32)).astype(jnp.bfloat16)
    q_four = block_q.reshape(blocks, length, HEADS, head_size).astype(jnp.float32)
    g_four = block_g.reshape(blocks, length, HEADS, head_size).astype(jnp.float32)
    k_four = keys.reshape(blocks, span, HEADS, head_size).astype(jnp.float32)
    v_four = values.reshape(blocks, span, HEADS, head_size).astype(jnp.float32)
    scores = jnp.einsum('bchd,brhd->bhcr', q_four, k_four) * scale
    top = lax.optimization_barrier(jnp.max(scores, axis=-1, keepdims=True))
    expo = jnp.exp(scores - top)
    prob = expo / lax.optimization_barrier(jnp.sum(expo, axis=-1, keepdims=True))
    prob_b = prob.astype(jnp.bfloat16)
    outputs = jnp.einsum('bhcr,brhd->bchd', prob_b.astype(jnp.float32), v_four).astype(jnp.bfloat16)
    dprob = jnp.einsum('bchd,brhd->bhcr', g_four, v_four)
    rowdot = lax.optimization_barrier(jnp.sum(prob * dprob, axis=-1, keepdims=True))
    dscore = (prob * (dprob - rowdot) * scale).astype(jnp.bfloat16).astype(jnp.float32)
    dquery = jnp.einsum('bhcr,brhd->bchd', dscore, k_four).astype(jnp.bfloat16)
    dkey = jnp.einsum('bhcr,bchd->brhd', dscore, q_four).astype(jnp.bfloat16).reshape(blocks, span, width)
    dvalue = jnp.einsum('bhcr,bchd->brhd', prob_b.astype(jnp.float32), g_four).astype(jnp.bfloat16).reshape(blocks, span, width)
    both = jnp.concatenate([dkey, dvalue], axis=-1)
    w_both = jnp.concatenate([w_key, w_value], axis=1)
    dstates = jnp.einsum('brf,ef->bre', both.astype(jnp.float32), w_both.astype(jnp.float32)).astype(jnp.bfloat16)
    return (outputs.reshape(blocks * length, width), dquery.reshape(blocks * length, width), both, dstates)

def reference(queries, cotangent, w_key, w_value, database, nb_shard, nb_row):
    width = HEADS * HSIZE
    total = DB_DEV * N_DB
    seq_count = queries.shape[0]
    length = queries.shape[1]
    stretch_count = length // STRETCH
    padding = jnp.zeros((seq_count, STRETCH - 1, width), queries.dtype)
    q_shift = jnp.concatenate([queries[:, STRETCH - 1:], padding], axis=1).reshape(seq_count, stretch_count, STRETCH, width)
    g_shift = jnp.concatenate([cotangent[:, STRETCH - 1:], padding], axis=1).reshape(seq_count, stretch_count, STRETCH, width)
    flat_ids = (nb_shard * DB_DEV + nb_row).astype(jnp.int32).reshape(seq_count, stretch_count * NEIGH)
    catalog = jnp.arange(total, dtype=jnp.int32)

    def per_sequence(carry, inputs):
        weight_sum, db_sum = carry
        block_q, block_g, idx = inputs
        states = jnp.take(database, idx, axis=0).reshape(stretch_count, NEIGH * NB_LEN, ENC)
        outputs, dquery, both, dstates = attend_blocks(block_q, block_g, states, w_key, w_value)
        weight_sum = weight_sum + jnp.einsum('bre,brf->ef', states.astype(jnp.float32), both.astype(jnp.float32))
        member = (idx[None, :] == catalog[:, None]).astype(jnp.float32)
        share = jnp.einsum('dk,kle->dle', member, dstates.reshape(stretch_count * NEIGH, NB_LEN, ENC).astype(jnp.float32))
        share = lax.optimization_barrier(share.astype(jnp.bfloat16))
        db_sum = db_sum + share.astype(jnp.float32)
        return ((weight_sum, db_sum), (outputs, dquery))
    start = (jnp.zeros((ENC, 2 * width), jnp.float32), jnp.zeros((total, NB_LEN, ENC), jnp.float32))
    (weight_sum, db_sum), (outs, dqs) = lax.scan(per_sequence, start, (q_shift, g_shift, flat_ids))
    leading = jnp.zeros((seq_count, STRETCH - 1, width), jnp.bfloat16)
    attn_out = jnp.concatenate([leading, outs[:, :length - STRETCH + 1]], axis=1)
    grad_queries = jnp.concatenate([leading, dqs[:, :length - STRETCH + 1]], axis=1)
    return (attn_out, grad_queries, weight_sum[:, :width], weight_sum[:, width:], db_sum.astype(jnp.bfloat16))
```

```python
import functools
import math

import jax
import jax.numpy as jnp
import numpy as np
from jax import lax
from jax.experimental import pallas as pl
from jax.experimental.pallas import tpu as pltpu
from jax.sharding import PartitionSpec as P

HSIZE = 128


def from_behind(block, axis, distance):
    devices = range(lax.axis_size(axis))
    route = [(i - distance, i) for i in devices if i - distance in devices]
    return lax.ppermute(block, axis, route)


def dot(a, b, dims):
    return lax.dot_general(a, b, (dims, ((), ())), preferred_element_type=jnp.float32)


def attend_kernel(scale, q_ref, g_ref, kv_ref, out_ref, dq_ref, both_ref):
    width = q_ref.shape[1]
    for head in range(width // HSIZE):
        cols = slice(head * HSIZE, (head + 1) * HSIZE)
        vcols = slice(width + head * HSIZE, width + (head + 1) * HSIZE)
        q = q_ref[:, cols]
        g = g_ref[:, cols]
        k = kv_ref[:, cols]
        v = kv_ref[:, vcols]
        scores = dot(q, k, ((1,), (1,))) * scale
        dprob = dot(g, v, ((1,), (1,)))
        expo = jnp.exp(scores - jnp.max(scores, axis=-1, keepdims=True))
        prob = expo * (1.0 / jnp.sum(expo, axis=-1, keepdims=True))
        prob_b = prob.astype(jnp.bfloat16)
        rowdot = jnp.sum(prob * dprob, axis=-1, keepdims=True)
        dscore = (prob * (dprob - rowdot) * scale).astype(jnp.bfloat16)
        out_ref[:, cols] = dot(prob_b, v, ((1,), (0,))).astype(jnp.bfloat16)
        dq_ref[:, cols] = dot(dscore, k, ((1,), (0,))).astype(jnp.bfloat16)
        both_ref[:, cols] = dot(dscore, q, ((0,), (0,))).astype(jnp.bfloat16)
        both_ref[:, vcols] = dot(prob_b, g, ((0,), (0,))).astype(jnp.bfloat16)


def attend(block_q, block_g, kv, stretches):
    rows, width = block_q.shape
    length = rows // stretches
    span = kv.shape[0] // stretches
    scale = 1.0 / math.sqrt(HSIZE)
    small = pl.BlockSpec((length, width), lambda u: (u, 0))
    large = pl.BlockSpec((span, 2 * width), lambda u: (u, 0))
    return pl.pallas_call(
        functools.partial(attend_kernel, scale),
        grid=(stretches,),
        in_specs=[small, small, large],
        out_specs=[small, small, large],
        out_shape=[
            jax.ShapeDtypeStruct((rows, width), jnp.bfloat16),
            jax.ShapeDtypeStruct((rows, width), jnp.bfloat16),
            jax.ShapeDtypeStruct(kv.shape, jnp.bfloat16),
        ],
        compiler_params=pltpu.CompilerParams(vmem_limit_bytes=40 << 20),
        cost_estimate=pl.CostEstimate(
            flops=12 * rows * span * width,
            bytes_accessed=8 * rows * width + 8 * kv.shape[0] * width,
            transcendentals=rows * span * width // HSIZE,
        ),
    )(block_q, block_g, kv)


def halve(block, axis, bit):
    size = lax.axis_size(axis)
    half = block.shape[0] // 2
    side = lax.rem(lax.axis_index(axis) // bit, 2)
    give = lax.dynamic_slice_in_dim(block, (1 - side) * half, half, 0)
    mine = lax.dynamic_slice_in_dim(block, side * half, half, 0)
    got = lax.ppermute(give, axis, [(i, i ^ bit) for i in range(size)])
    return mine.astype(jnp.float32) + got.astype(jnp.float32)


def bits_of(axis):
    size = lax.axis_size(axis)
    return [1 << b for b in range(size.bit_length() - 1)]


def halve_all(block, steps):
    for axis, bit in steps[:-1]:
        block = halve(block, axis, bit).astype(jnp.bfloat16)
    return halve(block, *steps[-1])


def reversed_order(count):
    bits = count.bit_length() - 1
    return np.array([int(format(i, "b").zfill(bits)[::-1], 2) if bits else 0 for i in range(count)])


def body(queries, cotangent, w_key, w_value, database, nb_shard, nb_row):
    q_local = queries[0]
    g_local = cotangent[0]
    rows_local, width = q_local.shape
    stretch_count = nb_shard.shape[1]
    neigh = nb_shard.shape[2]
    span = rows_local // stretch_count
    db_count, nb_len, enc_width = database.shape
    shards = lax.axis_size("db")
    seqs = lax.axis_size("dp")
    asks = stretch_count * neigh
    slot_count = 3 * asks // (2 * shards)
    target = nb_shard[0].reshape(asks)
    wanted = nb_row[0].reshape(asks)
    hits = (target[:, None] == jnp.arange(shards, dtype=jnp.int32)[None, :]).astype(jnp.int32)
    before = jnp.cumsum(hits, axis=0) - hits
    rank = jnp.sum(before * hits, axis=1)
    slot_pos = target * slot_count + rank
    place = (slot_pos[:, None] == jnp.arange(shards * slot_count, dtype=jnp.int32)[None, :]).astype(
        jnp.int32
    )
    send_ids = jnp.sum(place * wanted[:, None], axis=0).reshape(shards, slot_count)
    asked = lax.all_to_all(send_ids, "db", split_axis=0, concat_axis=0, tiled=True)
    picked = jnp.take(database, asked, axis=0)
    returned = lax.all_to_all(picked, "db", split_axis=0, concat_axis=0, tiled=True)

    ids = jnp.broadcast_to((target * db_count + wanted)[None], (seqs, asks))
    ids = lax.all_to_all(ids, "dp", split_axis=0, concat_axis=0, tiled=True).reshape(seqs * asks)
    member = (
        ids[None, :] == jnp.arange(shards * db_count, dtype=jnp.int32)[:, None]
    ).astype(jnp.bfloat16)

    next_q, next_g = from_behind((q_local[:span], g_local[:span]), "db", -1)
    block_q = jnp.concatenate([q_local[span - 1 :], next_q[: span - 1]], axis=0)
    block_g = jnp.concatenate([g_local[span - 1 :], next_g[: span - 1]], axis=0)
    w_both = jnp.concatenate([w_key, w_value], axis=1)

    devices = shards * seqs
    share = enc_width // devices
    source = (reversed_order(devices)[:, None] * share + np.arange(share)[None, :]).reshape(-1)
    shuffle = (
        jnp.arange(enc_width, dtype=jnp.int32)[:, None] == jnp.asarray(source, jnp.int32)[None, :]
    ).astype(jnp.bfloat16)

    states = jnp.take(returned.reshape(shards * slot_count, nb_len, enc_width), slot_pos, axis=0)
    states = states.reshape(asks * nb_len, enc_width)
    kv = dot(states, w_both, ((1,), (0,))).astype(jnp.bfloat16)
    shuffled = dot(states, shuffle, ((1,), (0,))).astype(jnp.bfloat16)
    outputs, dquery, both = attend(block_q, block_g, kv, stretch_count)

    steps = [("db", b) for b in bits_of("db")] + [("dp", b) for b in bits_of("dp")]
    grads = []
    for part in range(2):
        grad = dot(shuffled, both[:, part * width : (part + 1) * width], ((0,), (0,)))
        grads.append(halve_all(grad.astype(jnp.bfloat16), steps))

    keep = rows_local - span + 1
    prev_out, prev_dq = from_behind((outputs[keep:], dquery[keep:]), "db", 1)
    attn_out = jnp.concatenate([prev_out, outputs[:keep]], axis=0)[None]
    grad_queries = jnp.concatenate([prev_dq, dquery[:keep]], axis=0)[None]

    dstates = dot(both, w_both, ((1,), (1,))).astype(jnp.bfloat16)
    piece = nb_len // seqs
    dstates = dstates.reshape(asks, seqs, piece, enc_width).transpose(1, 0, 2, 3)
    arrived = lax.all_to_all(dstates, "dp", split_axis=0, concat_axis=0, tiled=True)
    dense = dot(member, arrived.reshape(seqs * asks, piece * enc_width), ((1,), (0,)))
    dense = dense.astype(jnp.bfloat16).reshape(shards, db_count, piece, enc_width)
    dense = dense[reversed_order(shards)]
    grad_database = halve_all(dense, [("db", b) for b in bits_of("db")])[0].astype(jnp.bfloat16)
    return (attn_out, grad_queries, grads[0], grads[1], grad_database)


def solution(mesh):
    return jax.shard_map(
        body,
        mesh=mesh,
        in_specs=(
            P("dp", "db", None),
            P("dp", "db", None),
            P(),
            P(),
            P("db", None, None),
            P("dp", "db", None),
            P("dp", "db", None),
        ),
        out_specs=(
            P("dp", "db", None),
            P("dp", "db", None),
            P(("dp", "db"), None),
            P(("dp", "db"), None),
            P("db", "dp", None),
        ),
        check_vma=False,
    )
```

```python
import functools
import math

import jax
import jax.numpy as jnp
import numpy as np
from jax import lax
from jax.experimental import pallas as pl
from jax.experimental.pallas import tpu as pltpu
from jax.sharding import PartitionSpec as P

HSIZE = 128


def from_behind(block, axis, distance):
    devices = range(lax.axis_size(axis))
    route = [(i - distance, i) for i in devices if i - distance in devices]
    return lax.ppermute(block, axis, route)


def dot(a, b, dims):
    return lax.dot_general(a, b, (dims, ((), ())), preferred_element_type=jnp.float32)


def attend_kernel(scale, q_ref, g_ref, kv_ref, out_ref, dq_ref, both_ref):
    width = q_ref.shape[1]
    for head in range(width // HSIZE):
        cols = slice(head * HSIZE, (head + 1) * HSIZE)
        vcols = slice(width + head * HSIZE, width + (head + 1) * HSIZE)
        q = q_ref[:, cols]
        g = g_ref[:, cols]
        k = kv_ref[:, cols]
        v = kv_ref[:, vcols]
        scores = dot(q, k, ((1,), (1,))) * scale
        dprob = dot(g, v, ((1,), (1,)))
        expo = jnp.exp(scores - jnp.max(scores, axis=-1, keepdims=True))
        prob = expo * (1.0 / jnp.sum(expo, axis=-1, keepdims=True))
        prob_b = prob.astype(jnp.bfloat16)
        rowdot = jnp.sum(prob * dprob, axis=-1, keepdims=True)
        dscore = (prob * (dprob - rowdot) * scale).astype(jnp.bfloat16)
        out_ref[:, cols] = dot(prob_b, v, ((1,), (0,))).astype(jnp.bfloat16)
        dq_ref[:, cols] = dot(dscore, k, ((1,), (0,))).astype(jnp.bfloat16)
        both_ref[:, cols] = dot(dscore, q, ((0,), (0,))).astype(jnp.bfloat16)
        both_ref[:, vcols] = dot(prob_b, g, ((0,), (0,))).astype(jnp.bfloat16)


def attend(block_q, block_g, kv, stretches):
    rows, width = block_q.shape
    length = rows // stretches
    span = kv.shape[0] // stretches
    scale = 1.0 / math.sqrt(HSIZE)
    small = pl.BlockSpec((length, width), lambda u: (u, 0))
    large = pl.BlockSpec((span, 2 * width), lambda u: (u, 0))
    return pl.pallas_call(
        functools.partial(attend_kernel, scale),
        grid=(stretches,),
        in_specs=[small, small, large],
        out_specs=[small, small, large],
        out_shape=[
            jax.ShapeDtypeStruct((rows, width), jnp.bfloat16),
            jax.ShapeDtypeStruct((rows, width), jnp.bfloat16),
            jax.ShapeDtypeStruct(kv.shape, jnp.bfloat16),
        ],
        compiler_params=pltpu.CompilerParams(vmem_limit_bytes=40 << 20),
        cost_estimate=pl.CostEstimate(
            flops=12 * rows * span * width,
            bytes_accessed=8 * rows * width + 8 * kv.shape[0] * width,
            transcendentals=rows * span * width // HSIZE,
        ),
    )(block_q, block_g, kv)


def halve(block, axis, bit):
    size = lax.axis_size(axis)
    half = block.shape[0] // 2
    side = lax.rem(lax.axis_index(axis) // bit, 2)
    give = lax.dynamic_slice_in_dim(block, (1 - side) * half, half, 0)
    mine = lax.dynamic_slice_in_dim(block, side * half, half, 0)
    got = lax.ppermute(give, axis, [(i, i ^ bit) for i in range(size)])
    return mine.astype(jnp.float32) + got.astype(jnp.float32)


def bits_of(axis):
    size = lax.axis_size(axis)
    return [1 << b for b in range(size.bit_length() - 1)]


def halve_all(block, steps):
    for axis, bit in steps[:-1]:
        block = halve(block, axis, bit).astype(jnp.bfloat16)
    return halve(block, *steps[-1])


def reversed_order(count):
    bits = count.bit_length() - 1
    return np.array([int(format(i, "b").zfill(bits)[::-1], 2) if bits else 0 for i in range(count)])


def finish_kernel(
    piece, lt_any, both_any, w_any, member_any, spread_ref,
    gk_ref, gv_ref, gd_ref,
    lt, both, wts, member, grad, got1, got2, got3, zed, got4, got5,
    dsend, arrived, give, dgot1, mine, xgive, dgot2,
    load_sem, send_sem, recv_sem, asend_sem, arecv_sem,
):
    bf, f32 = jnp.bfloat16, jnp.float32
    mesh_ids = pl.DeviceIdType.MESH
    dp, db = lax.axis_index("dp"), lax.axis_index("db")
    seqs = arrived.shape[0]
    c, x = lax.rem(db, 2), db // 2
    y, z0, z1 = lax.rem(dp, 2), lax.rem(dp // 2, 2), dp // 4
    pc = (dp, db + 1 - 2 * c)
    px = (dp, db + 2 - 4 * x)
    py = (dp + 1 - 2 * y, db)
    pz0 = (dp + 2 - 4 * z0, db)
    pz1 = (dp + 4 - 8 * z1, db)
    others = [(lax.rem(dp + d, seqs), db) for d in range(1, seqs)]
    loads = [
        pltpu.make_async_copy(lt_any, lt, load_sem.at[0]),
        pltpu.make_async_copy(both_any, both, load_sem.at[1]),
        pltpu.make_async_copy(w_any, wts, load_sem.at[2]),
        pltpu.make_async_copy(member_any, member, load_sem.at[3]),
    ]
    for load in loads:
        load.start()
    barrier = pltpu.get_barrier_semaphore()
    for peer in [pc, px] + others:
        pl.semaphore_signal(barrier, inc=1, device_id=peer, device_id_type=mesh_ids)
    pl.semaphore_wait(barrier, 2 + len(others))
    copies = []

    def send(src, dst, peer, sems=None):
        number = len(copies)
        copy = pltpu.make_async_remote_copy(
            src_ref=src,
            dst_ref=dst,
            send_sem=send_sem.at[number] if sems is None else asend_sem.at[sems],
            recv_sem=recv_sem.at[number] if sems is None else arecv_sem.at[sems],
            device_id=peer,
            device_id_type=mesh_ids,
        )
        copy.start()
        if sems is None:
            copies.append(copy)
        return copy

    def add(a, b):
        return (a.astype(f32) + b.astype(f32)).astype(bf)

    half = both.shape[1] // 2
    quarter = grad.shape[4]
    tile = 512

    def weight_grad(p):
        @pl.loop(0, half // tile)
        def _(t):
            cols = pl.ds(pl.multiple_of(p * half + t * tile, tile), tile)
            into = pl.ds(pl.multiple_of(t * tile, tile), tile)
            out = jnp.dot(lt[...], both[:, cols], preferred_element_type=f32).astype(bf)
            for b in range(8):
                grad[p, b // 4, b // 2 % 2, b % 2, :, into] = out[b * quarter : (b + 1) * quarter]

        return send(grad.at[p, 1 - c], got1.at[p], pc)

    def after_core(p, copy):
        copy.wait_recv()
        for i in range(2):
            for j in range(2):
                grad[p, c, i, j] = add(grad[p, c, i, j], got1[p, i, j])

    asked = dsend.shape[2] // piece
    rows = both.shape[0] // 2

    def states_grad(h):
        out = lax.dot_general(
            both[h * rows : (h + 1) * rows], wts[...], (((1,), (1,)), ((), ())),
            preferred_element_type=f32,
        ).astype(bf)
        for r in range(asked):
            for j in range(seqs):
                start = (r * seqs + j) * piece
                dsend[h, j, r * piece : (r + 1) * piece] = out[start : start + piece]
        arrived[dp, h] = dsend[h, dp]
        return [
            send(dsend.at[h, peer[0]], arrived.at[dp, h], peer, (h, d))
            for d, peer in enumerate(others)
        ]

    loads[0].wait()
    loads[1].wait()
    key1 = weight_grad(0)
    loads[2].wait()
    across = states_grad(0)
    after_core(0, key1)
    key2 = send(grad.at[0, c, 1 - x], got2.at[0], px)
    across += states_grad(1)
    value1 = weight_grad(1)
    after_core(1, value1)
    value2 = send(grad.at[1, c, :, 1 - y], got2.at[1], py)

    def expand(p, total):
        zed[p] = (
            jnp.dot(spread_ref[...], total, preferred_element_type=f32)
            .astype(bf)
            .reshape(zed.shape[1:])
        )
        return send(zed.at[p, 1 - z0], got4.at[p], pz0)

    key2.wait_recv()
    for j in range(2):
        grad[0, c, x, j] = add(grad[0, c, x, j], got2[0, j])
    key3 = send(grad.at[0, c, x, 1 - y], got3.at[0], py)
    value2.wait_recv()
    for i in range(2):
        grad[1, c, i, y] = add(grad[1, c, i, y], got2[1, i])
    value3 = send(grad.at[1, c, 1 - x, y], got3.at[1], px)
    key3.wait_recv()
    key4 = expand(0, add(grad[0, c, x, y], got3[0]))
    value3.wait_recv()
    value4 = expand(1, add(grad[1, c, x, y], got3[1]))

    for copy in across:
        copy.wait_recv()
    loads[3].wait()
    block = gd_ref.shape[0]
    every = arrived.shape[0] * arrived.shape[1] * arrived.shape[2]

    def dense(shard):
        return jnp.dot(
            member[pl.ds(pl.multiple_of(shard * block, block), block)],
            arrived[...].reshape(every, arrived.shape[3]),
            preferred_element_type=f32,
        )

    core = []
    for far in (1, 0):
        side = x if far == 0 else 1 - x
        give[far] = dense(2 * side + 1 - c).astype(bf)
        core.append(send(give.at[far], dgot1.at[far], pc))
    for far in (1, 0):
        side = x if far == 0 else 1 - x
        mine[far] = dense(2 * side + c)
    core[0].wait_recv()
    xgive[...] = (mine[1] + dgot1[1].astype(f32)).astype(bf)
    xcopy = send(xgive, dgot2, px)

    def last(p, copy):
        copy.wait_recv()
        for j in range(2):
            zed[p, z0, j] = add(zed[p, z0, j], got4[p, j])
        return send(zed.at[p, z0, 1 - z1], got5.at[p], pz1)

    key5 = last(0, key4)
    value5 = last(1, value4)
    core[1].wait_recv()
    mine[0] = mine[0] + dgot1[0].astype(f32)
    for p, copy, out_ref in ((0, key5, gk_ref), (1, value5, gv_ref)):
        copy.wait_recv()
        total = zed[p, z0, z1].astype(f32) + got5[p].astype(f32)
        out_ref[...] = total[: out_ref.shape[0]]
    xcopy.wait_recv()
    gd_ref[...] = (mine[0] + dgot2[...].astype(f32)).astype(bf)
    for copy in copies + across:
        copy.wait_send()


def finish(lt, both, w_both, member, spread, share, seqs, block, piece):
    enc, rows = lt.shape
    wide = both.shape[1]
    half = wide // 2
    quarter = enc // 8
    padded = spread.shape[0] // 4
    bf = jnp.bfloat16
    own = member.shape[1] // seqs
    anywhere = pl.BlockSpec(memory_space=pl.ANY)
    vmem = pl.BlockSpec(memory_space=pltpu.VMEM)
    return pl.pallas_call(
        functools.partial(finish_kernel, piece),
        in_specs=[anywhere] * 4 + [vmem],
        out_specs=[vmem] * 3,
        out_shape=[
            jax.ShapeDtypeStruct((share, half), jnp.float32),
            jax.ShapeDtypeStruct((share, half), jnp.float32),
            jax.ShapeDtypeStruct((block, enc), bf),
        ],
        scratch_shapes=[
            pltpu.VMEM(lt.shape, bf),
            pltpu.VMEM(both.shape, bf),
            pltpu.VMEM(w_both.shape, bf),
            pltpu.VMEM(member.shape, bf),
            pltpu.VMEM((2, 2, 2, 2, quarter, half), bf),
            pltpu.VMEM((2, 2, 2, quarter, half), bf),
            pltpu.VMEM((2, 2, quarter, half), bf),
            pltpu.VMEM((2, quarter, half), bf),
            pltpu.VMEM((2, 2, 2, padded, half), bf),
            pltpu.VMEM((2, 2, padded, half), bf),
            pltpu.VMEM((2, padded, half), bf),
            pltpu.VMEM((2, seqs, own // 2, enc), bf),
            pltpu.VMEM((seqs, 2, own // 2, enc), bf),
            pltpu.VMEM((2, block, enc), bf),
            pltpu.VMEM((2, block, enc), bf),
            pltpu.VMEM((2, block, enc), jnp.float32),
            pltpu.VMEM((block, enc), bf),
            pltpu.VMEM((block, enc), bf),
            pltpu.SemaphoreType.DMA((4,)),
            pltpu.SemaphoreType.DMA((16,)),
            pltpu.SemaphoreType.DMA((16,)),
            pltpu.SemaphoreType.DMA((2, seqs - 1)),
            pltpu.SemaphoreType.DMA((2, seqs - 1)),
        ],
        compiler_params=pltpu.CompilerParams(
            vmem_limit_bytes=62 << 20, collective_id=0, has_side_effects=True
        ),
    )(lt, both, w_both, member, spread)


def body(queries, cotangent, w_key, w_value, database, nb_shard, nb_row):
    q_local = queries[0]
    g_local = cotangent[0]
    rows_local, width = q_local.shape
    stretch_count = nb_shard.shape[1]
    neigh = nb_shard.shape[2]
    span = rows_local // stretch_count
    db_count, nb_len, enc_width = database.shape
    shards = lax.axis_size("db")
    seqs = lax.axis_size("dp")
    asks = stretch_count * neigh
    slot_count = 3 * asks // (2 * shards)
    target = nb_shard[0].reshape(asks)
    wanted = nb_row[0].reshape(asks)
    hits = (target[:, None] == jnp.arange(shards, dtype=jnp.int32)[None, :]).astype(jnp.int32)
    before = jnp.cumsum(hits, axis=0) - hits
    rank = jnp.sum(before * hits, axis=1)
    slot_pos = target * slot_count + rank
    place = (slot_pos[:, None] == jnp.arange(shards * slot_count, dtype=jnp.int32)[None, :]).astype(
        jnp.int32
    )
    send_ids = jnp.sum(place * wanted[:, None], axis=0).reshape(shards, slot_count)
    asked = lax.all_to_all(send_ids, "db", split_axis=0, concat_axis=0, tiled=True)
    picked = jnp.take(database, asked, axis=0, mode="clip")
    held, w_key, w_value, target, wanted = lax.optimization_barrier(
        (picked, w_key, w_value, target, wanted)
    )
    ids = jnp.broadcast_to((target * db_count + wanted)[None], (seqs, asks))
    ids = lax.all_to_all(ids, "dp", split_axis=0, concat_axis=0, tiled=True).reshape(seqs * asks)
    w_both = jnp.concatenate([w_key, w_value], axis=1)
    returned = lax.all_to_all(held, "db", split_axis=0, concat_axis=0, tiled=True)

    next_q, next_g = from_behind((q_local[:span], g_local[:span]), "db", -1)
    block_q = jnp.concatenate([q_local[span - 1 :], next_q[: span - 1]], axis=0)
    block_g = jnp.concatenate([g_local[span - 1 :], next_g[: span - 1]], axis=0)

    devices = shards * seqs
    share = enc_width // devices
    source = (reversed_order(devices)[:, None] * share + np.arange(share)[None, :]).reshape(-1)
    shuffle = (
        jnp.arange(enc_width, dtype=jnp.int32)[:, None] == jnp.asarray(source, jnp.int32)[None, :]
    ).astype(jnp.bfloat16)
    piece = nb_len // seqs
    fused = shards == 4 and seqs == 8
    if fused:
        row = jnp.arange(shards * db_count * piece, dtype=jnp.int32)[:, None]
        col = jnp.arange(seqs * asks * piece, dtype=jnp.int32)[None, :]
        member = (
            (jnp.broadcast_to(ids[:, None], (seqs * asks, piece)).reshape(1, -1) == row // piece) & (row % piece == col % piece)
        ).astype(jnp.bfloat16)
        padded = -(-share // 16) * 16
        row = jnp.arange(4 * padded, dtype=jnp.int32)[:, None]
        col = jnp.arange(4 * share, dtype=jnp.int32)[None, :]
        spread = ((row // padded == col // share) & (row % padded == col % share)).astype(
            jnp.bfloat16
        )
    else:
        member = (
            ids[None, :] == jnp.arange(shards * db_count, dtype=jnp.int32)[:, None]
        ).astype(jnp.bfloat16)

    states = jnp.take(returned.reshape(shards * slot_count, nb_len, enc_width), slot_pos, axis=0, mode="clip")
    states = states.reshape(asks * nb_len, enc_width)
    kv = dot(states, w_both, ((1,), (0,))).astype(jnp.bfloat16)
    outputs, dquery, both = attend(block_q, block_g, kv, stretch_count)

    keep = rows_local - span + 1
    prev_out, prev_dq = from_behind((outputs[keep:], dquery[keep:]), "db", 1)
    attn_out = jnp.concatenate([prev_out, outputs[:keep]], axis=0)[None]
    grad_queries = jnp.concatenate([prev_dq, dquery[:keep]], axis=0)[None]

    if fused:
        shuffled = dot(shuffle, states, ((0,), (1,))).astype(jnp.bfloat16)
        *grads, grad_database = finish(
            shuffled, both, w_both, member, spread, share, seqs, db_count * piece, piece
        )
        grad_database = grad_database.reshape(db_count, piece, enc_width)
        return (attn_out, grad_queries, grads[0], grads[1], grad_database)

    shuffled = dot(states, shuffle, ((1,), (0,))).astype(jnp.bfloat16)
    steps = [("db", b) for b in bits_of("db")] + [("dp", b) for b in bits_of("dp")]
    grads = []
    for part in range(2):
        grad = dot(shuffled, both[:, part * width : (part + 1) * width], ((0,), (0,)))
        grads.append(halve_all(grad.astype(jnp.bfloat16), steps))
    dstates = dot(both, w_both, ((1,), (1,))).astype(jnp.bfloat16)
    dstates = dstates.reshape(asks, seqs, piece, enc_width).transpose(1, 0, 2, 3)
    arrived = lax.all_to_all(dstates, "dp", split_axis=0, concat_axis=0, tiled=True)
    dense = dot(member, arrived.reshape(seqs * asks, piece * enc_width), ((1,), (0,)))
    dense = dense.astype(jnp.bfloat16).reshape(shards, db_count, piece, enc_width)
    dense = dense[reversed_order(shards)]
    grad_database = halve_all(dense, [("db", b) for b in bits_of("db")])[0].astype(jnp.bfloat16)
    return (attn_out, grad_queries, grads[0], grads[1], grad_database)


def solution(mesh):
    return jax.shard_map(
        body,
        mesh=mesh,
        in_specs=(
            P("dp", "db", None),
            P("dp", "db", None),
            P(),
            P(),
            P("db", None, None),
            P("dp", "db", None),
            P("dp", "db", None),
        ),
        out_specs=(
            P("dp", "db", None),
            P("dp", "db", None),
            P(("dp", "db"), None),
            P(("dp", "db"), None),
            P("db", "dp", None),
        ),
        check_vma=False,
    )
```

```python
import functools
import math

import jax
import jax.numpy as jnp
import numpy as np
from jax import lax
from jax.experimental import pallas as pl
from jax.experimental.pallas import tpu as pltpu
from jax.sharding import PartitionSpec as P

HSIZE = 128


def from_behind(block, axis, distance):
    devices = range(lax.axis_size(axis))
    route = [(i - distance, i) for i in devices if i - distance in devices]
    return lax.ppermute(block, axis, route)


def dot(a, b, dims):
    return lax.dot_general(a, b, (dims, ((), ())), preferred_element_type=jnp.float32)


def attend_kernel(scale, group, slot_ref, q_ref, g_ref, *refs):
    neigh = len(refs) - 6
    state_refs, (w_ref, shuffle_ref, out_ref, dq_ref, both_ref, lt_ref) = refs[:neigh], refs[neigh:]
    width = q_ref.shape[1]
    bf = jnp.bfloat16
    states = jnp.concatenate([ref[0] for ref in state_refs], axis=0)
    lt_ref[...] = dot(shuffle_ref[...], states, ((0,), (1,))).astype(bf)
    for first in range(0, width // HSIZE, group):
        many = slice(first * HSIZE, (first + group) * HSIZE)
        vmany = slice(width + first * HSIZE, width + (first + group) * HSIZE)
        keys = dot(states, w_ref[:, many], ((1,), (0,))).astype(bf)
        values = dot(states, w_ref[:, vmany], ((1,), (0,))).astype(bf)
        heads = range(group)
        local = [slice(h * HSIZE, (h + 1) * HSIZE) for h in heads]
        cols = [slice((first + h) * HSIZE, (first + h + 1) * HSIZE) for h in heads]
        vcols = [slice(width + (first + h) * HSIZE, width + (first + h + 1) * HSIZE) for h in heads]
        q = [q_ref[:, cols[h]] for h in heads]
        g = [g_ref[:, cols[h]] for h in heads]
        k = [keys[:, local[h]] for h in heads]
        v = [values[:, local[h]] for h in heads]
        scores = [dot(q[h], k[h], ((1,), (1,))) * scale for h in heads]
        dprob = [dot(g[h], v[h], ((1,), (1,))) for h in heads]
        expo = [jnp.exp(t - jnp.max(t, axis=-1, keepdims=True)) for t in scores]
        prob = [t * (1.0 / jnp.sum(t, axis=-1, keepdims=True)) for t in expo]
        rowdot = [jnp.sum(prob[h] * dprob[h], axis=-1, keepdims=True) for h in heads]
        dscore = [(prob[h] * (dprob[h] - rowdot[h]) * scale).astype(bf) for h in heads]
        prob_b = [t.astype(bf) for t in prob]
        for h in heads:
            out_ref[:, cols[h]] = dot(prob_b[h], v[h], ((1,), (0,))).astype(bf)
            dq_ref[:, cols[h]] = dot(dscore[h], k[h], ((1,), (0,))).astype(bf)
        for h in heads:
            both_ref[:, cols[h]] = dot(dscore[h], q[h], ((0,), (0,))).astype(bf)
            both_ref[:, vcols[h]] = dot(prob_b[h], g[h], ((0,), (0,))).astype(bf)


def attend(block_q, block_g, returned, slot_pos, w_both, shuffle, stretches):
    rows, width = block_q.shape
    length = rows // stretches
    asks = slot_pos.shape[0]
    neigh = asks // stretches
    _, nb_len, enc = returned.shape
    span = neigh * nb_len
    scale = 1.0 / math.sqrt(HSIZE)
    small = pl.BlockSpec((length, width), lambda u, slots: (u, 0))
    large = pl.BlockSpec((span, 2 * width), lambda u, slots: (u, 0))
    whole = lambda a: pl.BlockSpec(a.shape, lambda u, slots: (0, 0))
    fetched = [
        pl.BlockSpec((1, nb_len, enc), lambda u, slots, n=n: (slots[u * neigh + n], 0, 0))
        for n in range(neigh)
    ]
    return pl.pallas_call(
        functools.partial(attend_kernel, scale, 4),
        grid_spec=pltpu.PrefetchScalarGridSpec(
            num_scalar_prefetch=1,
            grid=(stretches,),
            in_specs=[small, small] + fetched + [whole(w_both), whole(shuffle)],
            out_specs=[small, small, large, pl.BlockSpec((enc, span), lambda u, slots: (0, u))],
        ),
        out_shape=[
            jax.ShapeDtypeStruct((rows, width), jnp.bfloat16),
            jax.ShapeDtypeStruct((rows, width), jnp.bfloat16),
            jax.ShapeDtypeStruct((asks * nb_len, 2 * width), jnp.bfloat16),
            jax.ShapeDtypeStruct((enc, asks * nb_len), jnp.bfloat16),
        ],
        compiler_params=pltpu.CompilerParams(vmem_limit_bytes=48 << 20),
        cost_estimate=pl.CostEstimate(
            flops=12 * rows * span * width + 4 * asks * nb_len * enc * width,
            bytes_accessed=8 * rows * width + 8 * asks * nb_len * width,
            transcendentals=rows * span * width // HSIZE,
        ),
    )(slot_pos, block_q, block_g, *[returned] * neigh, w_both, shuffle)


def halve(block, axis, bit):
    size = lax.axis_size(axis)
    half = block.shape[0] // 2
    side = lax.rem(lax.axis_index(axis) // bit, 2)
    give = lax.dynamic_slice_in_dim(block, (1 - side) * half, half, 0)
    mine = lax.dynamic_slice_in_dim(block, side * half, half, 0)
    got = lax.ppermute(give, axis, [(i, i ^ bit) for i in range(size)])
    return mine.astype(jnp.float32) + got.astype(jnp.float32)


def bits_of(axis):
    size = lax.axis_size(axis)
    return [1 << b for b in range(size.bit_length() - 1)]


def halve_all(block, steps):
    for axis, bit in steps[:-1]:
        block = halve(block, axis, bit).astype(jnp.bfloat16)
    return halve(block, *steps[-1])


def reversed_order(count):
    bits = count.bit_length() - 1
    return np.array([int(format(i, "b").zfill(bits)[::-1], 2) if bits else 0 for i in range(count)])


def finish_kernel(
    piece, lt_any, both_any, w_any, ids_ref, spread_ref,
    gk_ref, gv_ref, gd_ref,
    lt, both, wts, idbox, member, grad, got1, got2, got3, zed, got4, got5,
    dsend, arrived, give, dgot1, mine, xgive, dgot2,
    load_sem, send_sem, recv_sem, asend_sem, arecv_sem, isend_sem, irecv_sem,
):
    bf, f32 = jnp.bfloat16, jnp.float32
    mesh_ids = pl.DeviceIdType.MESH
    dp, db = lax.axis_index("dp"), lax.axis_index("db")
    seqs = arrived.shape[0]
    c, x = lax.rem(db, 2), db // 2
    y, z0, z1 = lax.rem(dp, 2), lax.rem(dp // 2, 2), dp // 4
    pc = (dp, db + 1 - 2 * c)
    px = (dp, db + 2 - 4 * x)
    py = (dp + 1 - 2 * y, db)
    pz0 = (dp + 2 - 4 * z0, db)
    pz1 = (dp + 4 - 8 * z1, db)
    others = [(lax.rem(dp + d, seqs), db) for d in range(1, seqs)]
    loads = [
        pltpu.make_async_copy(both_any, both, load_sem.at[1]),
        pltpu.make_async_copy(w_any, wts, load_sem.at[2]),
        pltpu.make_async_copy(lt_any, lt, load_sem.at[0]),
    ]
    for load in loads:
        load.start()
    barrier = pltpu.get_barrier_semaphore()
    for peer in [pc, px] + others:
        pl.semaphore_signal(barrier, inc=1, device_id=peer, device_id_type=mesh_ids)
    pl.semaphore_wait(barrier, 2 + len(others))
    copies = []

    def send(src, dst, peer, sems=None):
        number = len(copies)
        copy = pltpu.make_async_remote_copy(
            src_ref=src,
            dst_ref=dst,
            send_sem=send_sem.at[number] if sems is None else asend_sem.at[sems],
            recv_sem=recv_sem.at[number] if sems is None else arecv_sem.at[sems],
            device_id=peer,
            device_id_type=mesh_ids,
        )
        copy.start()
        if sems is None:
            copies.append(copy)
        return copy

    def add(a, b):
        return (a.astype(f32) + b.astype(f32)).astype(bf)

    half = both.shape[1] // 2
    quarter = grad.shape[4]
    tile = 512

    def weight_grad(p):
        @pl.loop(0, half // tile)
        def _(t):
            cols = pl.ds(pl.multiple_of(p * half + t * tile, tile), tile)
            into = pl.ds(pl.multiple_of(t * tile, tile), tile)
            out = jnp.dot(lt[...], both[:, cols], preferred_element_type=f32).astype(bf)
            for b in range(8):
                grad[p, b // 4, b // 2 % 2, b % 2, :, into] = out[b * quarter : (b + 1) * quarter]

        return send(grad.at[p, 1 - c], got1.at[p], pc)

    def after_core(p, copy):
        copy.wait_recv()
        for i in range(2):
            for j in range(2):
                grad[p, c, i, j] = add(grad[p, c, i, j], got1[p, i, j])

    asked = dsend.shape[1] // piece
    total = both.shape[0]
    enc = dsend.shape[2]
    cuts = [slice(0, 512), slice(512, enc)]

    def states_grad(h):
        cols = cuts[h]
        for part in range(2):
            rows = total // 2
            out = dot(both[part * rows : (part + 1) * rows], wts[cols], ((1,), (1,))).astype(bf)
            for r in range(asked // 2):
                into = (part * asked // 2 + r) * piece
                for j in range(seqs):
                    start = (r * seqs + j) * piece
                    dsend[j, into : into + piece, cols] = out[start : start + piece]
        arrived[dp, :, cols] = dsend[dp, :, cols]
        return [
            send(dsend.at[peer[0], :, cols], arrived.at[dp, :, cols], peer, (h, d))
            for d, peer in enumerate(others)
        ]

    idbox[dp] = ids_ref[...]
    named = []
    for d, peer in enumerate(others):
        copy = pltpu.make_async_remote_copy(
            src_ref=ids_ref,
            dst_ref=idbox.at[dp],
            send_sem=isend_sem.at[d],
            recv_sem=irecv_sem.at[d],
            device_id=peer,
            device_id_type=mesh_ids,
        )
        copy.start()
        named.append(copy)
    loads[0].wait()
    loads[1].wait()
    across = [states_grad(0), states_grad(1)]
    loads[2].wait()
    key1 = weight_grad(0)
    value1 = weight_grad(1)
    after_core(0, key1)
    key2 = send(grad.at[0, c, 1 - x], got2.at[0], px)
    after_core(1, value1)
    value2 = send(grad.at[1, c, :, 1 - y], got2.at[1], py)

    block = gd_ref.shape[0]
    lanes = member.shape[1] // seqs
    for copy in named:
        copy.wait_recv()
    row = lax.broadcasted_iota(jnp.int32, (block, lanes), 0)
    lane = lax.broadcasted_iota(jnp.int32, (block, lanes), 1)
    place = jnp.where(row % piece == lane % piece, row // piece, -1)
    for i in range(member.shape[0] // block):
        for k in range(seqs):
            hit = place == idbox[k][0:1] - i * (block // piece)
            member[i * block : (i + 1) * block, k * lanes : (k + 1) * lanes] = jnp.where(
                hit & (place >= 0), 1.0, 0.0
            ).astype(bf)

    def expand(p, total):
        zed[p] = (
            jnp.dot(spread_ref[...], total, preferred_element_type=f32)
            .astype(bf)
            .reshape(zed.shape[1:])
        )
        return send(zed.at[p, 1 - z0], got4.at[p], pz0)

    key2.wait_recv()
    for j in range(2):
        grad[0, c, x, j] = add(grad[0, c, x, j], got2[0, j])
    key3 = send(grad.at[0, c, x, 1 - y], got3.at[0], py)
    value2.wait_recv()
    for i in range(2):
        grad[1, c, i, y] = add(grad[1, c, i, y], got2[1, i])
    value3 = send(grad.at[1, c, 1 - x, y], got3.at[1], px)
    key3.wait_recv()
    key4 = expand(0, add(grad[0, c, x, y], got3[0]))
    value3.wait_recv()
    value4 = expand(1, add(grad[1, c, x, y], got3[1]))

    every = arrived.shape[0] * arrived.shape[1]

    def dense(shard, cols):
        return jnp.dot(
            member[pl.ds(pl.multiple_of(shard * block, block), block)],
            arrived[:, :, cols].reshape(every, cols.stop - cols.start),
            preferred_element_type=f32,
        )

    def core_start(h):
        cols = cuts[h]
        for copy in across[h]:
            copy.wait_recv()
        started = []
        for far in (1, 0):
            side = x if far == 0 else 1 - x
            give[far, :, cols] = dense(2 * side + 1 - c, cols).astype(bf)
            started.append(send(give.at[far, :, cols], dgot1.at[far, :, cols], pc))
        for far in (1, 0):
            side = x if far == 0 else 1 - x
            mine[far, :, cols] = dense(2 * side + c, cols)
        return started

    def x_start(h, started):
        cols = cuts[h]
        started[0].wait_recv()
        xgive[:, cols] = (mine[1, :, cols] + dgot1[1, :, cols].astype(f32)).astype(bf)
        copy = send(xgive.at[:, cols], dgot2.at[:, cols], px)
        started[1].wait_recv()
        mine[0, :, cols] = mine[0, :, cols] + dgot1[0, :, cols].astype(f32)
        return copy

    def last(p, copy):
        copy.wait_recv()
        for j in range(2):
            zed[p, z0, j] = add(zed[p, z0, j], got4[p, j])
        return send(zed.at[p, z0, 1 - z1], got5.at[p], pz1)

    xcopy = [x_start(0, core_start(0))]
    key5 = last(0, key4)
    value5 = last(1, value4)
    xcopy.append(x_start(1, core_start(1)))
    for p, copy, out_ref in ((0, key5, gk_ref), (1, value5, gv_ref)):
        copy.wait_recv()
        summed = zed[p, z0, z1].astype(f32) + got5[p].astype(f32)
        out_ref[...] = summed[: out_ref.shape[0]]
    for h in range(2):
        xcopy[h].wait_recv()
        cols = cuts[h]
        gd_ref[:, cols] = (mine[0, :, cols] + dgot2[:, cols].astype(f32)).astype(bf)
    for copy in copies + across[0] + across[1] + named:
        copy.wait_send()


def finish(lt, both, w_both, ids, spread, share, shards, seqs, block, piece):
    enc, rows = lt.shape
    wide = both.shape[1]
    half = wide // 2
    quarter = enc // 8
    padded = spread.shape[0] // 4
    bf = jnp.bfloat16
    own = ids.shape[1]
    anywhere = pl.BlockSpec(memory_space=pl.ANY)
    vmem = pl.BlockSpec(memory_space=pltpu.VMEM)
    return pl.pallas_call(
        functools.partial(finish_kernel, piece),
        in_specs=[anywhere] * 3 + [vmem] * 2,
        out_specs=[vmem] * 3,
        out_shape=[
            jax.ShapeDtypeStruct((share, half), jnp.float32),
            jax.ShapeDtypeStruct((share, half), jnp.float32),
            jax.ShapeDtypeStruct((block, enc), bf),
        ],
        scratch_shapes=[
            pltpu.VMEM(lt.shape, bf),
            pltpu.VMEM(both.shape, bf),
            pltpu.VMEM(w_both.shape, bf),
            pltpu.VMEM((seqs,) + ids.shape, jnp.int32),
            pltpu.VMEM((shards * block, seqs * own), bf),
            pltpu.VMEM((2, 2, 2, 2, quarter, half), bf),
            pltpu.VMEM((2, 2, 2, quarter, half), bf),
            pltpu.VMEM((2, 2, quarter, half), bf),
            pltpu.VMEM((2, quarter, half), bf),
            pltpu.VMEM((2, 2, 2, padded, half), bf),
            pltpu.VMEM((2, 2, padded, half), bf),
            pltpu.VMEM((2, padded, half), bf),
            pltpu.VMEM((seqs, own, enc), bf),
            pltpu.VMEM((seqs, own, enc), bf),
            pltpu.VMEM((2, block, enc), bf),
            pltpu.VMEM((2, block, enc), bf),
            pltpu.VMEM((2, block, enc), jnp.float32),
            pltpu.VMEM((block, enc), bf),
            pltpu.VMEM((block, enc), bf),
            pltpu.SemaphoreType.DMA((3,)),
            pltpu.SemaphoreType.DMA((16,)),
            pltpu.SemaphoreType.DMA((16,)),
            pltpu.SemaphoreType.DMA((2, seqs - 1)),
            pltpu.SemaphoreType.DMA((2, seqs - 1)),
            pltpu.SemaphoreType.DMA((seqs - 1,)),
            pltpu.SemaphoreType.DMA((seqs - 1,)),
        ],
        compiler_params=pltpu.CompilerParams(
            vmem_limit_bytes=62 << 20, collective_id=0, has_side_effects=True
        ),
    )(lt, both, w_both, ids, spread)


def body(queries, cotangent, w_key, w_value, database, nb_shard, nb_row):
    q_local = queries[0]
    g_local = cotangent[0]
    rows_local, width = q_local.shape
    stretch_count = nb_shard.shape[1]
    neigh = nb_shard.shape[2]
    span = rows_local // stretch_count
    db_count, nb_len, enc_width = database.shape
    shards = lax.axis_size("db")
    seqs = lax.axis_size("dp")
    asks = stretch_count * neigh
    slot_count = 3 * asks // (2 * shards)
    target = nb_shard[0].reshape(asks)
    wanted = nb_row[0].reshape(asks)
    hits = (target[:, None] == jnp.arange(shards, dtype=jnp.int32)[None, :]).astype(jnp.int32)
    before = jnp.cumsum(hits, axis=0) - hits
    rank = jnp.sum(before * hits, axis=1)
    slot_pos = target * slot_count + rank
    place = (slot_pos[:, None] == jnp.arange(shards * slot_count, dtype=jnp.int32)[None, :]).astype(
        jnp.int32
    )
    send_ids = jnp.sum(place * wanted[:, None], axis=0).reshape(shards, slot_count)
    asked = lax.all_to_all(send_ids, "db", split_axis=0, concat_axis=0, tiled=True)
    picked = jnp.take(database, asked, axis=0, mode="clip")
    held, w_key, w_value, target, wanted = lax.optimization_barrier(
        (picked, w_key, w_value, target, wanted)
    )
    own_ids = target * db_count + wanted
    w_both = jnp.concatenate([w_key, w_value], axis=1)
    returned = lax.all_to_all(held, "db", split_axis=0, concat_axis=0, tiled=True)

    next_q, next_g = from_behind((q_local[:span], g_local[:span]), "db", -1)
    block_q = jnp.concatenate([q_local[span - 1 :], next_q[: span - 1]], axis=0)
    block_g = jnp.concatenate([g_local[span - 1 :], next_g[: span - 1]], axis=0)

    devices = shards * seqs
    share = enc_width // devices
    source = (reversed_order(devices)[:, None] * share + np.arange(share)[None, :]).reshape(-1)
    shuffle = (
        jnp.arange(enc_width, dtype=jnp.int32)[:, None] == jnp.asarray(source, jnp.int32)[None, :]
    ).astype(jnp.bfloat16)
    piece = nb_len // seqs
    fused = shards == 4 and seqs == 8
    if fused:
        ids = jnp.broadcast_to(own_ids[:, None], (asks, piece)).reshape(1, asks * piece)
        ids = jnp.broadcast_to(ids, (8, asks * piece))
        padded = -(-share // 16) * 16
        row = jnp.arange(4 * padded, dtype=jnp.int32)[:, None]
        col = jnp.arange(4 * share, dtype=jnp.int32)[None, :]
        spread = ((row // padded == col // share) & (row % padded == col % share)).astype(
            jnp.bfloat16
        )
    else:
        ids = jnp.broadcast_to(own_ids[None], (seqs, asks))
        ids = lax.all_to_all(ids, "dp", split_axis=0, concat_axis=0, tiled=True)
        ids = ids.reshape(seqs * asks)
        member = (
            ids[None, :] == jnp.arange(shards * db_count, dtype=jnp.int32)[:, None]
        ).astype(jnp.bfloat16)

    returned = returned.reshape(shards * slot_count, nb_len, enc_width)
    outputs, dquery, both, lt = attend(
        block_q, block_g, returned, slot_pos, w_both, shuffle, stretch_count
    )

    keep = rows_local - span + 1
    prev_out, prev_dq = from_behind((outputs[keep:], dquery[keep:]), "db", 1)
    attn_out = jnp.concatenate([prev_out, outputs[:keep]], axis=0)[None]
    grad_queries = jnp.concatenate([prev_dq, dquery[:keep]], axis=0)[None]

    if fused:
        *grads, grad_database = finish(
            lt, both, w_both, ids, spread, share, shards, seqs, db_count * piece, piece
        )
        grad_database = grad_database.reshape(db_count, piece, enc_width)
        return (attn_out, grad_queries, grads[0], grads[1], grad_database)

    steps = [("db", b) for b in bits_of("db")] + [("dp", b) for b in bits_of("dp")]
    grads = []
    for part in range(2):
        grad = dot(lt, both[:, part * width : (part + 1) * width], ((1,), (0,)))
        grads.append(halve_all(grad.astype(jnp.bfloat16), steps))
    dstates = dot(both, w_both, ((1,), (1,))).astype(jnp.bfloat16)
    dstates = dstates.reshape(asks, seqs, piece, enc_width).transpose(1, 0, 2, 3)
    arrived = lax.all_to_all(dstates, "dp", split_axis=0, concat_axis=0, tiled=True)
    dense = dot(member, arrived.reshape(seqs * asks, piece * enc_width), ((1,), (0,)))
    dense = dense.astype(jnp.bfloat16).reshape(shards, db_count, piece, enc_width)
    dense = dense[reversed_order(shards)]
    grad_database = halve_all(dense, [("db", b) for b in bits_of("db")])[0].astype(jnp.bfloat16)
    return (attn_out, grad_queries, grads[0], grads[1], grad_database)


def solution(mesh):
    return jax.shard_map(
        body,
        mesh=mesh,
        in_specs=(
            P("dp", "db", None),
            P("dp", "db", None),
            P(),
            P(),
            P("db", None, None),
            P("dp", "db", None),
            P("dp", "db", None),
        ),
        out_specs=(
            P("dp", "db", None),
            P("dp", "db", None),
            P(("dp", "db"), None),
            P(("dp", "db"), None),
            P("db", "dp", None),
        ),
        check_vma=False,
    )
```
